1024 devices in a mesh: ctx: 16 (over y, core), chan: 64 (over x, z).
Axes of the slice: x: 4, y: 8, z: 16, core: 2. Of those that a mesh axis runs over, the one named last changes fastest.
Arguments:
- features: float32 [3, 2048, 8192], P(None, 'ctx', 'chan'), may hold values from -6 to 6
- saved_conv: float32 [2048, 8192], P('ctx', 'chan'), may hold values from -6 to 6
- out_grad: float32 [2048, 8192], P('ctx', 'chan'), may hold values from -16 to 16
- short_filter: float32 [3, 3, 8192], P(None, None, 'chan'), may hold values from -3 to 3
- residue: float32 [8192, 16], P('chan'), may hold values from -0.18 to 0.18
- rate: float32 [8192, 16], P('chan'), may hold values from 4.8828125e-05 to 0.0333333333
- bias: float32 [8192], P('chan'), may hold values from -1 to 1
- w_proj: bfloat16 [3, 8192, 8192], P(None, 'chan'), may hold values from -0.0625 to 0.0625
Outputs:
- grad_inputs: float32 [3, 2048, 8192], P(None, 'ctx', 'chan')
- grad_x: float32 [2048, 8192], P('ctx', 'chan')
- grad_residue: float32 [8192, 16], P('chan')
- grad_bias: float32 [8192], P('chan')
The draws below stay inside these ranges and needn't reach their ends.
All inputs are finite; a program needn't handle non-finite values.
Results may differ from the reference program's by a relative error of at most 0.0029.
Values may be sent and summed in bfloat16 or wider, within the bound.
A program may use at most 64 MiB of HBM per device.

```python
import jax
import jax.numpy as jnp
from jax import lax

D = 8192
MODES = 16
TOKENS = 2048


def draw_rate(key, part):
    lower = jnp.log(0.1 / TOKENS)
    upper = jnp.log(1.0 / 30.0)
    spread = jax.random.uniform(key, (D, MODES), jnp.float32)
    return jnp.exp(lower + spread * (upper - lower)).astype(jnp.float32)


def strengthened(drawn, own_key, source, target, parts, factor):
    def block_of(dim):
        return (jnp.arange(drawn.shape[dim]) // (drawn.shape[dim] // parts)).reshape((-1,) + (1,) * (drawn.ndim - 1 - dim))

    first = jax.random.permutation(own_key, parts)[block_of(target)]
    second = (block_of(target) + parts // 2) % parts
    return jnp.where((block_of(source) == first) | (block_of(source) == second), factor * drawn, drawn)


def steps_of(stream_key, dims, shards, low, high):
    loudness = 1.0
    for position, parts in shards:
        draws = jax.random.uniform(jax.random.fold_in(jax.random.fold_in(stream_key, 6), position), (parts,), jnp.float32, low / len(shards), high / len(shards))
        loudness = loudness * jnp.repeat(jnp.exp(draws), dims[position] // parts).reshape((-1,) + (1,) * (len(dims) - 1 - position))
    return loudness


def gaussian(stream_key, extent, deviation, bound, pieces=(), kind=jnp.bfloat16):
    level = steps_of(stream_key, extent, pieces, -0.22, 0.18) if pieces else 1.0
    array = jax.random.normal(stream_key, extent, jnp.float32) * deviation * level
    return jnp.minimum(jnp.maximum(array, -bound), bound).astype(kind)


def gaussian_with(key, shape, scale, reach, cuts, heavy, dtype=jnp.bfloat16):
    array = scale * jax.random.normal(key, shape, jnp.float32)
    if cuts:
        array = array * steps_of(key, shape, cuts, -0.22, 0.18)
    return jnp.clip(strengthened(array, jax.random.fold_in(key, 3), *heavy), -reach, reach).astype(dtype)


def setup_inputs(seed: int = 0) -> dict:
    key_of = jax.random.split(jax.random.key(seed), 9)
    features = gaussian(key_of[0], (3, TOKENS, D), 1.0, 6.0, ((1, 16), (2, 64)), jnp.float32)
    saved_conv = gaussian(key_of[1], (TOKENS, D), 1.0, 6.0, ((0, 16), (1, 64)), jnp.float32)
    out_grad = gaussian_with(key_of[2], (TOKENS, D), 1.0, 16.0, ((0, 16), (1, 64)), (1, 0, 64, 4.0), jnp.float32)
    short_filter = gaussian(key_of[3], (3, 3, D), 0.6, 3.0, ((2, 64),), jnp.float32)
    residue = gaussian(key_of[4], (D, MODES), 0.03, 0.18, ((0, 64),), jnp.float32)
    rate = draw_rate(jax.random.fold_in(key_of[8], 71), 0)
    bias = jnp.clip(jax.random.uniform(key_of[6], (D,), jnp.float32, -1.0, 1.0) * steps_of(key_of[6], (D,), ((0, 64),), -0.4, 0.0), -1.0, 1.0)
    w_proj = gaussian(key_of[7], (3, D, D), D ** -0.5, 0.0625, ((1, 64),))
    return {"features": features, "saved_conv": saved_conv, "out_grad": out_grad, "short_filter": short_filter, "residue": residue, "rate": rate, "bias": bias, "w_proj": w_proj}


def reference(features, saved_conv, out_grad, short_filter, residue, rate, bias, w_proj):
    gate_feat = features[0]
    key_feat = features[1]
    value_feat = features[2]
    product = key_feat * value_feat
    signal = out_grad * gate_feat
    grad_gate = out_grad * (saved_conv + bias * product)
    decay = jnp.exp(-rate)

    def backward_step(carry, inputs):
        state, accum = carry
        sig_row, prod_row = inputs
        state = sig_row[:, None] + decay * state
        accum = accum + prod_row[:, None] * state
        return (state, accum), jnp.sum(residue * state, axis=1)

    zeros = jnp.zeros(rate.shape, jnp.float32)
    (final_state, accum), corr = lax.scan(backward_step, (zeros, zeros), (signal, product), reverse=True)
    grad_prod = corr + bias * signal
    grad_stream = jnp.stack([grad_gate, grad_prod * value_feat, grad_prod * key_feat])
    padded = jnp.pad(grad_stream, ((0, 0), (0, 2), (0, 0)))
    grad_inputs = short_filter[:, 0][:, None, :] * padded[:, 0:TOKENS]
    grad_inputs = grad_inputs + short_filter[:, 1][:, None, :] * padded[:, 1:TOKENS + 1]
    grad_inputs = grad_inputs + short_filter[:, 2][:, None, :] * padded[:, 2:TOKENS + 2]
    rounded = grad_inputs.astype(jnp.bfloat16)
    grad_x = jnp.dot(rounded[0], w_proj[0].T, preferred_element_type=jnp.float32)
    grad_x = grad_x + jnp.dot(rounded[1], w_proj[1].T, preferred_element_type=jnp.float32)
    grad_x = grad_x + jnp.dot(rounded[2], w_proj[2].T, preferred_element_type=jnp.float32)
    scale = TOKENS ** -0.5
    grad_residue = accum * scale
    grad_bias = jnp.sum(signal * product, axis=0) * scale
    return grad_inputs, grad_x, grad_residue, grad_bias
```

```python
import jax
import jax.numpy as jnp
from jax import lax
from jax.experimental import pallas as pl
from jax.experimental.pallas import tpu as pltpu
from jax.sharding import PartitionSpec as P

NX = 4
MODES = 16
TOK = 128
LANES = 128
SHARES = 4
F32 = jnp.float32
BF16 = jnp.bfloat16
MESH = pl.DeviceIdType.MESH


def make_kernel(nctx, nz):
    ny = nctx // 2
    half = nz // 2
    width = nz * LANES
    share_rows = LANES // SHARES
    half_rows = share_rows // 2
    scale = (TOK * nctx) ** -0.5
    blocks = TOK // 8

    def kernel(feat, sconv, ograd, sfilt, residue, rate, bias, w,
               gi_out, gx_out, gr_out, gb_out,
               feat_v, sc_v, og_v, sf_v, res_v, rate_v, bias_v, sig_v, prod_v, corr_v, gs_v,
               base_v, d8_v, z_v, fsend, frecv, halo, gsend, grecv, abuf, wbuf, relay,
               acc_v, csend, crecv,
               in_sem, w_sem, f_ssem, f_rsem, h_ssem, h_rsem, g_ssem, g_rsem,
               a_ssem, a_rsem, b_ssem, b_rsem, c_ssem, c_rsem):
        ctx = lax.axis_index("ctx")
        chan = lax.axis_index("chan")
        x = chan // nz
        z = lax.rem(chan, nz)
        y = ctx // 2
        core = lax.rem(ctx, 2)

        def at_x(dx):
            return {"chan": lax.rem(x + dx + NX, NX) * nz + z}

        def at_z(dz):
            return {"chan": x * nz + lax.rem(z + dz + nz, nz)}

        def at_ctx(c):
            return {"ctx": c}

        def at_y(dy):
            return {"ctx": lax.rem(y + dy + ny, ny) * 2 + core}

        other = at_ctx(y * 2 + 1 - core)
        sign = 1 - 2 * core

        def remote(src, dst, ssem, rsem, device):
            return pltpu.make_async_remote_copy(
                src_ref=src, dst_ref=dst, send_sem=ssem, recv_sem=rsem,
                device_id=device, device_id_type=MESH)

        barrier = pltpu.get_barrier_semaphore()

        def greet(d, carry):
            pl.semaphore_signal(barrier, inc=1, device_id=at_ctx(lax.rem(ctx + d, nctx)),
                                device_id_type=MESH)
            return carry

        lax.fori_loop(1, nctx, greet, 0)
        for dx in range(1, NX):
            pl.semaphore_signal(barrier, inc=1, device_id=at_x(dx), device_id_type=MESH)
        for dz in (1, -1):
            pl.semaphore_signal(barrier, inc=1, device_id=at_z(dz), device_id_type=MESH)

        loads = [pltpu.make_async_copy(s, d, in_sem.at[i]) for i, (s, d) in enumerate((
            (feat, feat_v), (ograd, og_v), (rate, rate_v), (residue, res_v), (sconv, sc_v),
            (sfilt, sf_v), (bias, bias_v)))]
        for c in loads:
            c.start()
        own_rows = pl.ds(pl.multiple_of(x * LANES, LANES), LANES)
        own_w = pltpu.make_async_copy(
            w.at[:, :, pl.ds(pl.multiple_of(x * width, LANES), width)],
            wbuf.at[:, own_rows, :], w_sem.at[0])
        own_w.start()
        for c in loads:
            c.wait()

        sig_v[...] = og_v[...] * feat_v[0]
        prod_v[...] = feat_v[1] * feat_v[2]

        iota8 = lax.broadcasted_iota(jnp.int32, (8, LANES), 0).astype(F32)
        for m in range(MODES):
            rm = jnp.broadcast_to(rate_v[m:m + 1, :], (8, LANES))
            d8 = jnp.exp(rm * -8.0)
            up = jnp.exp(-rm * iota8)
            base_v[m] = jnp.exp(-rm * (8.0 - iota8))
            d8_v[m] = d8
            total = jnp.zeros((8, LANES), F32)
            for k in range(blocks):
                total = total + up * sig_v[8 * k:8 * k + 8, :]
                up = up * d8
            fsend[m:m + 1, :] = jnp.sum(total, axis=0, keepdims=True)

        pl.semaphore_wait(barrier, nctx - 1 + NX - 1 + 2)

        prev = at_ctx(lax.rem(ctx + nctx - 1, nctx))
        halo_copies = [
            remote(feat.at[:, 0:8, :], halo.at[0:3], h_ssem.at[0], h_rsem.at[0], prev),
            remote(ograd.at[0:8, :], halo.at[3], h_ssem.at[1], h_rsem.at[1], prev),
            remote(sconv.at[0:8, :], halo.at[4], h_ssem.at[2], h_rsem.at[2], prev)]
        for c in halo_copies:
            c.start()

        def f_copy(src_ctx, dst):
            return remote(fsend, frecv.at[src_ctx], f_ssem.at[dst], f_rsem.at[src_ctx], at_ctx(dst))

        def send_f(i, carry):
            f_copy(ctx, i).start()
            return carry

        lax.fori_loop(0, ctx, send_f, 0)

        share = 2 * lax.rem(y, 2) + core
        r0 = share * share_rows

        def rows_of(dx, first, count):
            return pl.ds(pl.multiple_of(lax.rem(x + dx + NX, NX) * LANES + first, 8), count)

        def cols_of(dx):
            return pl.ds(pl.multiple_of(lax.rem(x + dx + NX, NX) * width, LANES), width)

        mine = pl.ds(pl.multiple_of(r0, 8), share_rows)
        mine0 = pl.ds(pl.multiple_of(r0, 8), half_rows)
        mine1 = pl.ds(pl.multiple_of(r0 + half_rows, 8), half_rows)
        here = wbuf.at[:, rows_of(0, r0, share_rows), :]
        b_out0 = remote(w.at[:, mine0, cols_of(2)], relay.at[0], b_ssem.at[2], b_rsem.at[2], at_x(1))
        b_out1 = remote(w.at[:, mine1, cols_of(2)], relay.at[1], b_ssem.at[3], b_rsem.at[3], at_x(-1))
        b_right = remote(w.at[:, mine, cols_of(1)], here, b_ssem.at[0], b_rsem.at[0], at_x(1))
        b_left = remote(w.at[:, mine, cols_of(-1)], here, b_ssem.at[1], b_rsem.at[1], at_x(-1))
        for c in (b_out0, b_out1, b_right, b_left):
            c.start()
        b_relay0 = remote(relay.at[0], wbuf.at[:, rows_of(-1, r0, half_rows), :],
                          b_ssem.at[4], b_rsem.at[4], at_x(1))
        b_relay1 = remote(relay.at[1], wbuf.at[:, rows_of(1, r0 + half_rows, half_rows), :],
                          b_ssem.at[5], b_rsem.at[5], at_x(-1))

        def same_place(dx, first, count, sem, device):
            ref = wbuf.at[:, rows_of(dx, first, count), :]
            return remote(ref, ref, b_ssem.at[sem], b_rsem.at[sem], device)

        dec = jnp.exp(-rate_v[...])
        res = res_v[...]

        def scan_block(i, carry):
            state, total = carry
            first = pl.multiple_of(TOK - 8 - 8 * i, 8)
            sig8 = sig_v[pl.ds(first, 8), :]
            prod8 = prod_v[pl.ds(first, 8), :]
            rows = [None] * 8
            for t in range(7, -1, -1):
                state = sig8[t:t + 1, :] + dec * state
                total = total + prod8[t:t + 1, :] * state
                rows[t] = jnp.sum(res * state, axis=0, keepdims=True)
            corr_v[pl.ds(first, 8), :] = jnp.concatenate(rows, axis=0)
            return state, total

        zero = jnp.zeros((MODES, LANES), F32)
        _, near_grad = lax.fori_loop(0, blocks, scan_block, (zero, zero))

        for m in range(MODES):
            down = base_v[m]
            d8 = d8_v[m]
            total = jnp.zeros((8, LANES), F32)
            for k in range(blocks - 1, -1, -1):
                total = total + down * prod_v[8 * k:8 * k + 8, :]
                down = down * d8
            z_v[m:m + 1, :] = jnp.sum(total, axis=0, keepdims=True)

        bias_row = bias_v[...]
        for c in halo_copies:
            c.wait_recv()
        keep = jnp.logical_and(ctx < nctx - 1, lax.broadcasted_iota(jnp.int32, (8, LANES), 0) < 2)
        sig_h = halo[3] * halo[0]
        prod_h = halo[1] * halo[2]
        gs_v[0, TOK:TOK + 8, :] = jnp.where(keep, halo[3] * (halo[4] + bias_row * prod_h), 0.0)
        gs_v[0, 0:TOK, :] = og_v[...] * (sc_v[...] + bias_row * prod_v[...])

        own_cols = pl.ds(pl.multiple_of(z * LANES, LANES), LANES)

        def finish_stream(p):
            taps = sf_v[p]
            g = taps[0:1, :] * gs_v[p, 0:TOK, :]
            g = g + taps[1:2, :] * gs_v[p, 1:TOK + 1, :]
            g = g + taps[2:3, :] * gs_v[p, 2:TOK + 2, :]
            gi_out[p] = g
            abuf[p, :, own_cols] = g.astype(BF16)

        def slot_cols(d):
            return pl.ds(pl.multiple_of(lax.rem(z + d + nz, nz) * LANES, LANES), LANES)

        def a_copy(way, step, p):
            heading = sign if way == 0 else -sign
            ref = abuf.at[p, :, slot_cols(-heading * step)]
            return remote(ref, ref, a_ssem.at[way, step, p], a_rsem.at[way, step, p], at_z(heading))

        def start_own(p):
            a_copy(0, 0, p).start()
            if half > 1:
                a_copy(1, 0, p).start()

        finish_stream(0)
        start_own(0)

        d128 = jnp.exp(-rate_v[...] * float(TOK))

        def join(i, state):
            s = nctx - 1 - i
            f_copy(s, ctx).wait_recv()
            return frecv[s] + d128 * state

        state_in = lax.fori_loop(0, nctx - 1 - ctx, join, zero)

        q = res * state_in
        far = [jnp.zeros((8, LANES), F32) for _ in range(blocks)]
        for m in range(MODES):
            cur = q[m:m + 1, :] * base_v[m]
            d8 = d8_v[m]
            for k in range(blocks - 1, -1, -1):
                far[k] = far[k] + cur
                if k:
                    cur = cur * d8
        corr = corr_v[...] + jnp.concatenate(far, axis=0)
        corr_h0 = jnp.sum(q, axis=0, keepdims=True)
        state_h1 = (state_in - sig_h[0:1, :]) * jnp.exp(rate_v[...])
        corr_h1 = jnp.sum(res * state_h1, axis=0, keepdims=True)
        first_row = lax.broadcasted_iota(jnp.int32, (8, LANES), 0) == 0
        gp_h = jnp.where(first_row, corr_h0, corr_h1) + bias_row * sig_h
        gp = corr + bias_row * sig_v[...]
        gs_v[1, TOK:TOK + 8, :] = jnp.where(keep, gp_h * halo[2], 0.0)
        gs_v[1, 0:TOK, :] = gp * feat_v[2]
        finish_stream(1)
        start_own(1)
        gs_v[2, TOK:TOK + 8, :] = jnp.where(keep, gp_h * halo[1], 0.0)
        gs_v[2, 0:TOK, :] = gp * feat_v[1]
        finish_stream(2)
        start_own(2)

        gsend[0:MODES, :] = near_grad + state_in * z_v[...]
        gsend[MODES:MODES + 8, :] = jnp.broadcast_to(
            jnp.sum(sig_v[...] * prod_v[...], axis=0, keepdims=True), (8, LANES))

        def g_copy(src_ctx, dst):
            return remote(gsend, grecv.at[src_ctx], g_ssem.at[dst], g_rsem.at[src_ctx], at_ctx(dst))

        def send_g(d, carry):
            g_copy(ctx, lax.rem(ctx + d, nctx)).start()
            return carry

        lax.fori_loop(1, nctx, send_g, 0)

        def ring(lo, hi):
            def step_body(step, carry):
                for p in range(3):
                    a_copy(0, step, p).wait_recv()

                    @pl.when(step < half - 1)
                    def _():
                        a_copy(0, step + 1, p).start()

                    @pl.when(step < half - 1)
                    def _():
                        a_copy(1, step, p).wait_recv()

                    @pl.when(step < half - 2)
                    def _():
                        a_copy(1, step + 1, p).start()
                return carry

            lax.fori_loop(lo, hi, step_body, 0)

        marks = [min(half, m) for m in (2, 4, 7, 8)]
        ring(0, marks[0])
        b_out0.wait_recv()
        b_relay0.start()
        b_out1.wait_recv()
        b_relay1.start()
        ring(marks[0], marks[1])

        b_in = [b_right, b_left, b_relay0, b_relay1]
        core_out = [same_place(-1, r0, share_rows, 6, other), same_place(1, r0, share_rows, 7, other),
                    same_place(2, r0, half_rows, 8, other), same_place(2, r0 + half_rows, half_rows, 9, other)]
        y_out = [[same_place(-1, r0, half_rows, 10, at_y(1)), same_place(-1, r0 + half_rows, half_rows, 11, at_y(-1))],
                 [same_place(1, r0, half_rows, 12, at_y(1)), same_place(1, r0 + half_rows, half_rows, 13, at_y(-1))],
                 [same_place(2, r0, half_rows, 14, at_y(1))],
                 [same_place(2, r0 + half_rows, half_rows, 15, at_y(-1))]]
        ry = (2 * (1 - lax.rem(y, 2)) + core) * share_rows
        yc_out = []
        for j, dx in enumerate((-1, 1, 2)):
            yc_out.append(same_place(dx, ry, half_rows, 16 + 2 * j, other))
            yc_out.append(same_place(dx, ry + half_rows, half_rows, 17 + 2 * j, other))
        y_in = [y_out[0][0], y_out[0][1], y_out[1][0], y_out[1][1], y_out[2][0], y_out[3][0]]

        def pass_on(i):
            b_in[i].wait_recv()
            for c in y_out[i]:
                c.start()
            core_out[i].start()

        pass_on(0)
        pass_on(1)
        ring(marks[1], marks[2])
        for i in range(4):
            y_in[i].wait_recv()
            yc_out[i].start()
        pass_on(2)
        pass_on(3)
        ring(marks[2], marks[3])
        for i in range(4, 6):
            y_in[i].wait_recv()
            yc_out[i].start()
        for c in core_out + yc_out:
            c.wait_recv()
        own_w.wait()

        dims = (((1,), (1,)), ((), ()))
        acc = lax.dot_general(abuf[0], wbuf[0], dims, preferred_element_type=F32)
        acc = acc + lax.dot_general(abuf[1], wbuf[1], dims, preferred_element_type=F32)
        acc_v[...] = acc + lax.dot_general(abuf[2], wbuf[2], dims, preferred_element_type=F32)

        def piece(dx):
            return acc_v[:, pl.ds(pl.multiple_of(lax.rem(x + dx, NX) * LANES, LANES), LANES)]

        c_copies = []
        for dx in (2, 1, 3):
            csend[dx - 1] = piece(dx).astype(BF16)
            c = remote(csend.at[dx - 1], crecv.at[dx - 1], c_ssem.at[dx - 1], c_rsem.at[dx - 1], at_x(dx))
            c.start()
            c_copies.append(c)

        def g_wait(d, total):
            s = lax.rem(ctx + d, nctx)
            g_copy(s, ctx).wait_recv()
            return total + grecv[s]

        total = lax.fori_loop(1, nctx, g_wait, gsend[...])
        gr_out[...] = total[0:MODES, :] * scale
        gb_out[...] = total[MODES:MODES + 1, :] * scale

        for c in c_copies:
            c.wait_recv()
        gx_out[...] = ((piece(0) + crecv[0].astype(F32)) + crecv[1].astype(F32)) + crecv[2].astype(F32)

        for c in halo_copies + [b_out0, b_out1, b_right, b_left, b_relay0, b_relay1] + core_out + yc_out + y_in + c_copies:
            c.wait_send()

        def f_sent(i, carry):
            f_copy(ctx, i).wait_send()
            return carry

        lax.fori_loop(0, ctx, f_sent, 0)

        def g_sent(d, carry):
            g_copy(ctx, lax.rem(ctx + d, nctx)).wait_send()
            return carry

        lax.fori_loop(1, nctx, g_sent, 0)

        def a_sent(step, carry):
            for p in range(3):
                a_copy(0, step, p).wait_send()

                @pl.when(step < half - 1)
                def _():
                    a_copy(1, step, p).wait_send()
            return carry

        lax.fori_loop(0, half, a_sent, 0)

    return kernel


def build(nctx, nchan):
    nz = nchan // NX
    half = nz // 2
    width = nz * LANES
    half_rows = LANES // SHARES // 2
    any_spec = pl.BlockSpec(memory_space=pl.ANY)
    vmem_spec = pl.BlockSpec(memory_space=pltpu.VMEM)
    dma = pltpu.SemaphoreType.DMA
    vm = pltpu.VMEM
    call = pl.pallas_call(
        make_kernel(nctx, nz),
        out_shape=(
            jax.ShapeDtypeStruct((3, TOK, LANES), F32),
            jax.ShapeDtypeStruct((TOK, LANES), F32),
            jax.ShapeDtypeStruct((MODES, LANES), F32),
            jax.ShapeDtypeStruct((1, LANES), F32)),
        in_specs=[any_spec] * 8,
        out_specs=(vmem_spec,) * 4,
        scratch_shapes=[
            vm((3, TOK, LANES), F32), vm((TOK, LANES), F32), vm((TOK, LANES), F32),
            vm((3, 3, LANES), F32), vm((MODES, LANES), F32), vm((MODES, LANES), F32), vm((1, LANES), F32),
            vm((TOK, LANES), F32), vm((TOK, LANES), F32), vm((TOK, LANES), F32), vm((3, TOK + 8, LANES), F32),
            vm((MODES, 8, LANES), F32), vm((MODES, 8, LANES), F32), vm((MODES, LANES), F32),
            vm((MODES, LANES), F32), vm((nctx, MODES, LANES), F32), vm((5, 8, LANES), F32),
            vm((MODES + 8, LANES), F32), vm((nctx, MODES + 8, LANES), F32),
            vm((3, TOK, width), BF16), vm((3, NX * LANES, width), BF16), vm((2, 3, half_rows, width), BF16),
            vm((TOK, NX * LANES), F32), vm((NX - 1, TOK, LANES), BF16), vm((NX - 1, TOK, LANES), BF16),
            dma((7,)), dma((1,)), dma((nctx,)), dma((nctx,)), dma((3,)), dma((3,)), dma((nctx,)), dma((nctx,)),
            dma((2, half, 3)), dma((2, half, 3)), dma((22,)), dma((22,)), dma((3,)), dma((3,))],
        compiler_params=pltpu.CompilerParams(
            collective_id=0, has_side_effects=True, vmem_limit_bytes=40 * 1024 * 1024),
    )

    def body(features, saved_conv, out_grad, short_filter, residue, rate, bias, w_proj):
        gi, gx, gr, gb = call(
            features, saved_conv, out_grad, short_filter, residue.T, rate.T, bias.reshape(1, LANES), w_proj)
        return gi, gx, gr.T, gb.reshape(LANES)

    return body


def solution(mesh):
    return jax.shard_map(
        build(mesh.shape["ctx"], mesh.shape["chan"]),
        mesh=mesh,
        in_specs=(
            P(None, "ctx", "chan"),
            P("ctx", "chan"),
            P("ctx", "chan"),
            P(None, None, "chan"),
            P("chan", None),
            P("chan", None),
            P("chan"),
            P(None, "chan", None),
        ),
        out_specs=(P(None, "ctx", "chan"), P("ctx", "chan"), P("chan", None), P("chan")),
        check_vma=False,
    )
```

```python
import jax
import jax.numpy as jnp
from jax import lax
from jax.experimental import pallas as pl
from jax.experimental.pallas import tpu as pltpu
from jax.sharding import PartitionSpec as P

NX = 4
MODES = 16
TOK = 128
LANES = 128
SHARES = 4
PARTS = ((0, 0, 16), (1, 0, 16), (2, 0, 8), (2, 8, 4), (2, 12, 4))
X_START, HOP, A_START = 7.7, 3.0, (9.0, 13.0, 13.3)
JUMP = (4, 4, 4)
EARLY = 1
F32 = jnp.float32
BF16 = jnp.bfloat16
MESH = pl.DeviceIdType.MESH


def make_kernel(nctx, nz):
    ny = nctx // 2
    half = nz // 2
    strides = [way * d for d in sorted({1} | {j for j in JUMP if j <= half}) for way in (1, -1)]
    width = nz * LANES
    part = width // 16
    share_rows = LANES // SHARES
    half_rows = share_rows // 2
    scale = (TOK * nctx) ** -0.5
    blocks = TOK // 8

    def kernel(feat, sconv, ograd, sfilt, residue, rate, bias, w,
               gi_out, gx_out, gr_out, gb_out,
               feat_v, sc_v, og_v, sf_v, res_v, rate_v, bias_v, sig_v, prod_v, corr_v, gs_v,
               base_v, d8_v, z_v, fsend, frecv, halo, gsum, grecv, abuf, wbuf,
               acc_v, csend, crecv,
               in_sem, w_sem, f_ssem, f_rsem, h_ssem, h_rsem, g_ssem, g_rsem,
               a_ssem, a_rsem, b_ssem, b_rsem, c_ssem, c_rsem):
        ctx = lax.axis_index("ctx")
        chan = lax.axis_index("chan")
        x = chan // nz
        z = lax.rem(chan, nz)
        y = ctx // 2
        core = lax.rem(ctx, 2)

        def at_x(dx):
            return {"chan": lax.rem(x + dx + NX, NX) * nz + z}

        def at_z(dz):
            return {"chan": x * nz + lax.rem(z + dz + nz, nz)}

        def at_ctx(c):
            return {"ctx": c}

        def at_y(dy):
            return {"ctx": lax.rem(y + dy + ny, ny) * 2 + core}

        other = at_ctx(y * 2 + 1 - core)
        sign = 1 - 2 * core

        def remote(src, dst, ssem, rsem, device):
            return pltpu.make_async_remote_copy(
                src_ref=src, dst_ref=dst, send_sem=ssem, recv_sem=rsem,
                device_id=device, device_id_type=MESH)

        barrier = pltpu.get_barrier_semaphore()

        def greet(d, carry):
            pl.semaphore_signal(barrier, inc=1, device_id=at_ctx(lax.rem(ctx + d, nctx)),
                                device_id_type=MESH)
            return carry

        lax.fori_loop(1, nctx, greet, 0)
        for dx in range(1, NX):
            pl.semaphore_signal(barrier, inc=1, device_id=at_x(dx), device_id_type=MESH)
        for dz in strides:
            pl.semaphore_signal(barrier, inc=1, device_id=at_z(dz), device_id_type=MESH)

        loads = [pltpu.make_async_copy(s, d, in_sem.at[i]) for i, (s, d) in enumerate((
            (feat, feat_v), (ograd, og_v), (rate, rate_v), (residue, res_v), (sconv, sc_v),
            (sfilt, sf_v), (bias, bias_v)))]
        for c in loads:
            c.start()
        own_rows = pl.ds(pl.multiple_of(x * LANES, LANES), LANES)
        own_w = pltpu.make_async_copy(
            w.at[:, :, pl.ds(pl.multiple_of(x * width, LANES), width)],
            wbuf.at[:, own_rows, :], w_sem.at[0])
        own_w.start()
        for c in loads:
            c.wait()

        sig_v[...] = og_v[...] * feat_v[0]
        prod_v[...] = feat_v[1] * feat_v[2]

        iota8 = lax.broadcasted_iota(jnp.int32, (8, LANES), 0).astype(F32)
        for m in range(MODES):
            rm = jnp.broadcast_to(rate_v[m:m + 1, :], (8, LANES))
            d8 = jnp.exp(rm * -8.0)
            up = jnp.exp(-rm * iota8)
            base_v[m] = jnp.exp(-rm * (8.0 - iota8))
            d8_v[m] = d8
            total = jnp.zeros((8, LANES), F32)
            for k in range(blocks):
                total = total + up * sig_v[8 * k:8 * k + 8, :]
                up = up * d8
            fsend[m:m + 1, :] = jnp.sum(total, axis=0, keepdims=True)

        pl.semaphore_wait(barrier, nctx - 1 + NX - 1 + len(strides))

        prev = at_ctx(lax.rem(ctx + nctx - 1, nctx))
        halo_copies = [
            remote(feat.at[:, 0:8, :], halo.at[0:3], h_ssem.at[0], h_rsem.at[0], prev),
            remote(ograd.at[0:8, :], halo.at[3], h_ssem.at[1], h_rsem.at[1], prev),
            remote(sconv.at[0:8, :], halo.at[4], h_ssem.at[2], h_rsem.at[2], prev)]

        def f_copy(src_ctx, dst):
            return remote(fsend, frecv.at[src_ctx], f_ssem.at[dst], f_rsem.at[src_ctx], at_ctx(dst))

        for dy in sorted(range(1, ny), key=lambda d: -min(d, ny - d)):
            @pl.when(y >= dy)
            def _():
                f_copy(ctx, (y - dy) * 2 + core).start()
                f_copy(ctx, (y - dy) * 2 + 1 - core).start()

        @pl.when(core == 1)
        def _():
            f_copy(ctx, y * 2).start()

        for c in halo_copies:
            c.start()

        share = 2 * lax.rem(y, 2) + core
        r0 = share * share_rows

        def rows_of(dx, first, count):
            return pl.ds(pl.multiple_of(lax.rem(x + dx + NX, NX) * LANES + first, 8), count)

        def cols_of(dx, q):
            first = lax.rem(x + dx + NX, NX) * width + PARTS[q][1] * part
            return pl.ds(pl.multiple_of(first, LANES), PARTS[q][2] * part)

        mine = pl.ds(pl.multiple_of(r0, 8), share_rows)
        ry = (2 * (1 - lax.rem(y, 2)) + core) * share_rows
        towards = (2, 1, -1)
        origin = (2, -1, 1)

        def b_fetch(q, j):
            return remote(w.at[PARTS[q][0], mine, cols_of(towards[j], q)],
                          wbuf.at[PARTS[q][0], rows_of(0, r0, share_rows), cols_in(q)],
                          b_ssem.at[0, q, j], b_rsem.at[0, q, j], at_x(towards[j]))

        def cols_in(q):
            return pl.ds(PARTS[q][1] * part, PARTS[q][2] * part)

        def same_place(kind, q, j, first, count, device):
            ref = wbuf.at[PARTS[q][0], rows_of(origin[j], first, count), cols_in(q)]
            return remote(ref, ref, b_ssem.at[kind, q, j], b_rsem.at[kind, q, j], device)

        def b_core(p, j):
            return same_place(1, p, j, r0, share_rows, other)

        def b_up(p, j):
            return same_place(2, p, j, r0, half_rows, at_y(1))

        def b_down(p, j):
            return same_place(3, p, j, r0 + half_rows, half_rows, at_y(-1))

        def b_up_in(p, j):
            return same_place(2, p, j, ry, half_rows, at_y(1))

        def b_down_in(p, j):
            return same_place(3, p, j, ry + half_rows, half_rows, at_y(-1))

        def b_core2(p, j):
            return same_place(4, p, j, ry, share_rows, other)

        pieces = [(q, j) for q in range(len(PARTS)) for j in range(3)]
        for p, j in pieces:
            b_fetch(p, j).start()

        def fetched(p, j):
            b_fetch(p, j).wait_recv()
            b_up(p, j).start()
            b_down(p, j).start()
            b_core(p, j).start()

        def from_y(p, j):
            b_up_in(p, j).wait_recv()
            b_down_in(p, j).wait_recv()
            b_core2(p, j).start()

        dec = jnp.exp(-rate_v[...])
        res = res_v[...]

        def scan_block(i, carry):
            state, total = carry
            first = pl.multiple_of(TOK - 8 - 8 * i, 8)
            sig8 = sig_v[pl.ds(first, 8), :]
            prod8 = prod_v[pl.ds(first, 8), :]
            rows = [None] * 8
            for t in range(7, -1, -1):
                state = sig8[t:t + 1, :] + dec * state
                total = total + prod8[t:t + 1, :] * state
                rows[t] = jnp.sum(res * state, axis=0, keepdims=True)
            corr_v[pl.ds(first, 8), :] = jnp.concatenate(rows, axis=0)
            return state, total

        zero = jnp.zeros((MODES, LANES), F32)
        _, near_grad = lax.fori_loop(0, blocks, scan_block, (zero, zero))

        for m in range(MODES):
            down = base_v[m]
            d8 = d8_v[m]
            total = jnp.zeros((8, LANES), F32)
            for k in range(blocks - 1, -1, -1):
                total = total + down * prod_v[8 * k:8 * k + 8, :]
                down = down * d8
            z_v[m:m + 1, :] = jnp.sum(total, axis=0, keepdims=True)

        bias_row = bias_v[...]
        for c in halo_copies:
            c.wait_recv()
        keep = jnp.logical_and(ctx < nctx - 1, lax.broadcasted_iota(jnp.int32, (8, LANES), 0) < 2)
        sig_h = halo[3] * halo[0]
        prod_h = halo[1] * halo[2]
        gs_v[0, TOK:TOK + 8, :] = jnp.where(keep, halo[3] * (halo[4] + bias_row * prod_h), 0.0)
        gs_v[0, 0:TOK, :] = og_v[...] * (sc_v[...] + bias_row * prod_v[...])

        def finish_stream(p):
            taps = sf_v[p]
            g = taps[0:1, :] * gs_v[p, 0:TOK, :]
            g = g + taps[1:2, :] * gs_v[p, 1:TOK + 1, :]
            g = g + taps[2:3, :] * gs_v[p, 2:TOK + 2, :]
            gi_out[p] = g
            abuf[z, p] = g.astype(BF16)

        reach = (half, half - 1)

        def a_send(way, dist, p):
            heading = sign if way == 0 else -sign
            hops = dist if dist == JUMP[p] else 1
            ref = abuf.at[lax.rem(z - heading * (dist - hops) + nz, nz), p]
            return remote(ref, ref, a_ssem.at[way, dist, p], a_rsem.at[way, dist, p], at_z(heading * hops))

        def a_recv(way, dist, p):
            heading = sign if way == 0 else -sign
            ref = abuf.at[lax.rem(z - heading * dist + nz, nz), p]
            return remote(ref, ref, a_ssem.at[way, dist, p], a_rsem.at[way, dist, p], at_z(heading))

        def start_own(p):
            for dist in sorted({1, JUMP[p]}, reverse=True):
                for way in range(2):
                    if dist <= reach[way]:
                        a_send(way, dist, p).start()

        def passes(way, dist, p):
            return dist + 1 <= reach[way] and dist + 1 != JUMP[p]

        def ring(p, dist):
            for way in range(2):
                if passes(way, dist, p):
                    a_recv(way, dist, p).wait_recv()
                    a_send(way, dist + 1, p).start()

        def ring_ends(p):
            for way in range(2):
                for dist in range(1, reach[way] + 1):
                    if not passes(way, dist, p):
                        a_recv(way, dist, p).wait_recv()

        finish_stream(0)
        start_own(0)

        for dist in range(1, EARLY + 1):
            ring(0, dist)

        d128 = jnp.exp(-rate_v[...] * float(TOK))

        def join(i, state):
            s = nctx - 1 - i
            f_copy(s, ctx).wait_recv()
            return frecv[s] + d128 * state

        state_in = lax.fori_loop(0, nctx - 1 - ctx, join, zero)

        q = res * state_in
        far = [jnp.zeros((8, LANES), F32) for _ in range(blocks)]
        for m in range(MODES):
            cur = q[m:m + 1, :] * base_v[m]
            d8 = d8_v[m]
            for k in range(blocks - 1, -1, -1):
                far[k] = far[k] + cur
                if k:
                    cur = cur * d8
        corr = corr_v[...] + jnp.concatenate(far, axis=0)
        corr_h0 = jnp.sum(q, axis=0, keepdims=True)
        state_h1 = (state_in - sig_h[0:1, :]) * jnp.exp(rate_v[...])
        corr_h1 = jnp.sum(res * state_h1, axis=0, keepdims=True)
        first_row = lax.broadcasted_iota(jnp.int32, (8, LANES), 0) == 0
        gp_h = jnp.where(first_row, corr_h0, corr_h1) + bias_row * sig_h
        gp = corr + bias_row * sig_v[...]
        gs_v[1, TOK:TOK + 8, :] = jnp.where(keep, gp_h * halo[2], 0.0)
        gs_v[1, 0:TOK, :] = gp * feat_v[2]
        finish_stream(1)
        start_own(1)
        gs_v[2, TOK:TOK + 8, :] = jnp.where(keep, gp_h * halo[1], 0.0)
        gs_v[2, 0:TOK, :] = gp * feat_v[1]
        finish_stream(2)
        start_own(2)

        gsum[0, 0:MODES, :] = near_grad + state_in * z_v[...]
        gsum[0, MODES:MODES + 8, :] = jnp.broadcast_to(
            jnp.sum(sig_v[...] * prod_v[...], axis=0, keepdims=True), (8, LANES))

        g_pair = remote(gsum.at[0], grecv.at[ny], g_ssem.at[0], g_rsem.at[0], other)
        g_pair.start()

        def g_copy(src, dy):
            return remote(gsum.at[1], grecv.at[src], g_ssem.at[dy], g_rsem.at[1 + src], at_y(dy))

        def g_chip():
            g_pair.wait_recv()
            chip = gsum[0] + grecv[ny]
            gsum[1] = chip
            grecv[y] = chip
            for dy in range(1, ny):
                g_copy(y, dy).start()

        events = []
        for dist in range(1, half + 1):
            for p in range(3):
                took = HOP * (dist if dist < JUMP[p] else dist - JUMP[p] + 0.7 + 0.3 * JUMP[p])
                if p or dist > EARLY:
                    events.append((A_START[p] + took, lambda p=p, dist=dist: ring(p, dist)))
        before = 0
        for q, (_, _, size) in enumerate(PARTS):
            for j in range(3):
                at = X_START + 18.3 / 48 * (before + size * (0.8, 0.95, 1.0)[j])
                events.append((at, lambda q=q, j=j: fetched(q, j)))
                events.append((at + 3.0 + 13.7 / 48 * size, lambda q=q, j=j: from_y(q, j)))
            before += size
        events.append((A_START[2] + 3.0, g_chip))
        for _, act in sorted(events, key=lambda e: e[0]):
            act()

        own_w.wait()
        dims = (((1,), (1,)), ((), ()))

        def product_of(p):
            for q, j in pieces:
                if PARTS[q][0] == p:
                    b_core(q, j).wait_recv()
                    b_core2(q, j).wait_recv()
            ring_ends(p)
            column = jnp.concatenate([abuf[slot, p] for slot in range(nz)], axis=1)
            return lax.dot_general(column, wbuf[p], dims, preferred_element_type=F32)

        acc_v[...] = product_of(0) + product_of(1)
        acc_v[...] += product_of(2)

        def piece(dx):
            return acc_v[:, pl.ds(pl.multiple_of(lax.rem(x + dx, NX) * LANES, LANES), LANES)]

        c_copies = []
        for dx in (2, 1, 3):
            csend[dx - 1] = piece(dx).astype(BF16)
            c = remote(csend.at[dx - 1], crecv.at[dx - 1], c_ssem.at[dx - 1], c_rsem.at[dx - 1], at_x(dx))
            c.start()
            c_copies.append(c)

        for src in range(1, ny):
            s = lax.rem(y + src, ny)
            g_copy(s, src).wait_recv()
        total = grecv[0]
        for src in range(1, ny):
            total = total + grecv[src]
        gr_out[...] = total[0:MODES, :] * scale
        gb_out[...] = total[MODES:MODES + 1, :] * scale

        for c in c_copies:
            c.wait_recv()
        gx_out[...] = ((piece(0) + crecv[0].astype(F32)) + crecv[1].astype(F32)) + crecv[2].astype(F32)

        for c in halo_copies + c_copies:
            c.wait_send()
        for p, j in pieces:
            for make in (b_fetch, b_core, b_up, b_down, b_core2):
                make(p, j).wait_send()
        g_pair.wait_send()
        for dy in range(1, ny):
            g_copy(y, dy).wait_send()

        def f_sent(i, carry):
            f_copy(ctx, i).wait_send()
            return carry

        lax.fori_loop(0, ctx, f_sent, 0)

        for p in range(3):
            for way in range(2):
                for dist in range(1, reach[way] + 1):
                    a_send(way, dist, p).wait_send()

    return kernel


def build(nctx, nchan):
    nz = nchan // NX
    half = nz // 2
    width = nz * LANES
    ny = nctx // 2
    any_spec = pl.BlockSpec(memory_space=pl.ANY)
    vmem_spec = pl.BlockSpec(memory_space=pltpu.VMEM)
    dma = pltpu.SemaphoreType.DMA
    vm = pltpu.VMEM
    shapes = (
        jax.ShapeDtypeStruct((3, TOK, LANES), F32),
        jax.ShapeDtypeStruct((TOK, LANES), F32),
        jax.ShapeDtypeStruct((MODES, LANES), F32),
        jax.ShapeDtypeStruct((1, LANES), F32))
    call = pl.pallas_call(
        make_kernel(nctx, nz),
        out_shape=shapes,
        in_specs=[any_spec] * 8,
        out_specs=(vmem_spec,) * 4,
        scratch_shapes=[
            vm((3, TOK, LANES), F32), vm((TOK, LANES), F32), vm((TOK, LANES), F32),
            vm((3, 3, LANES), F32), vm((MODES, LANES), F32), vm((MODES, LANES), F32), vm((1, LANES), F32),
            vm((TOK, LANES), F32), vm((TOK, LANES), F32), vm((TOK, LANES), F32), vm((3, TOK + 8, LANES), F32),
            vm((MODES, 8, LANES), F32), vm((MODES, 8, LANES), F32), vm((MODES, LANES), F32),
            vm((MODES, LANES), F32), vm((nctx, MODES, LANES), F32), vm((5, 8, LANES), F32),
            vm((2, MODES + 8, LANES), F32), vm((ny + 1, MODES + 8, LANES), F32),
            vm((nz, 3, TOK, LANES), BF16), vm((3, NX * LANES, width), BF16),
            vm((TOK, NX * LANES), F32), vm((NX - 1, TOK, LANES), BF16), vm((NX - 1, TOK, LANES), BF16),
            dma((7,)), dma((1,)), dma((nctx,)), dma((nctx,)), dma((3,)), dma((3,)), dma((ny,)), dma((ny + 1,)),
            dma((2, nz // 2 + 1, 3)), dma((2, nz // 2 + 1, 3)), dma((5, len(PARTS), 3)), dma((5, len(PARTS), 3)), dma((3,)), dma((3,))],
        compiler_params=pltpu.CompilerParams(
            collective_id=0, has_side_effects=True, vmem_limit_bytes=40 * 1024 * 1024),
    )

    def put_out_kernel(*refs):
        sources, targets, sem = refs[:4], refs[4:8], refs[8]
        copies = [pltpu.make_async_copy(a, b, sem.at[i]) for i, (a, b) in enumerate(zip(sources, targets))]
        for c in copies:
            c.start()
        for c in copies:
            c.wait()

    put_out = pl.pallas_call(
        put_out_kernel,
        out_shape=shapes,
        in_specs=[vmem_spec] * 4,
        out_specs=(any_spec,) * 4,
        scratch_shapes=[dma((4,))],
        compiler_params=pltpu.CompilerParams(vmem_limit_bytes=8 * 1024 * 1024),
    )

    def body(features, saved_conv, out_grad, short_filter, residue, rate, bias, w_proj):
        operands = (features, saved_conv, out_grad, short_filter, residue.T, rate.T, bias.reshape(1, LANES), w_proj)
        gi, gx, gr, gb = put_out(*call(*[pltpu.with_memory_space_constraint(v, pltpu.HBM) for v in operands]))
        return gi, gx, gr.T, gb.reshape(LANES)

    return body


def solution(mesh):
    return jax.shard_map(
        build(mesh.shape["ctx"], mesh.shape["chan"]),
        mesh=mesh,
        in_specs=(
            P(None, "ctx", "chan"),
            P("ctx", "chan"),
            P("ctx", "chan"),
            P(None, None, "chan"),
            P("chan", None),
            P("chan", None),
            P("chan"),
            P(None, "chan", None),
        ),
        out_specs=(P(None, "ctx", "chan"), P("ctx", "chan"), P("chan", None), P("chan")),
        check_vma=False,
    )
```

```python
import jax
import jax.numpy as jnp
from jax import lax
from jax.experimental import pallas as pl
from jax.experimental.pallas import tpu as pltpu
from jax.sharding import PartitionSpec as P

NX = 4
MODES = 16
TOK = 128
LANES = 128
SHARES = 4
PARTS = ((0, 0, 16), (1, 0, 16), (2, 0, 8), (2, 8, 4), (2, 12, 4))
X_START, HOP, A_START = 7.7, 4.0, (9.0, 13.0, 13.3)
JUMP = (4, 4, 4)
EARLY = 1
F32 = jnp.float32
BF16 = jnp.bfloat16
MESH = pl.DeviceIdType.MESH


def make_kernel(nctx, nz):
    ny = nctx // 2
    half = nz // 2
    strides = [way * d for d in sorted({1} | {j for j in JUMP if j <= half}) for way in (1, -1)]
    width = nz * LANES
    part = width // 16
    share_rows = LANES // SHARES
    half_rows = share_rows // 2
    scale = (TOK * nctx) ** -0.5
    blocks = TOK // 8

    def kernel(feat, sconv, ograd, sfilt, residue, rate, bias, w,
               gi_out, gx_out, gr_out, gb_out,
               feat_v, sc_v, og_v, sf_v, res_v, rate_v, bias_v, sig_v, prod_v, corr_v, gs_v,
               base_v, d8_v, z_v, fsend, frecv, halo, gsum, grecv, abuf, wbuf,
               acc_v, csend, crecv,
               in_sem, w_sem, f_ssem, f_rsem, h_ssem, h_rsem, g_ssem, g_rsem,
               a_ssem, a_rsem, b_ssem, b_rsem, c_ssem, c_rsem):
        ctx = lax.axis_index("ctx")
        chan = lax.axis_index("chan")
        x = chan // nz
        z = lax.rem(chan, nz)
        y = ctx // 2
        core = lax.rem(ctx, 2)

        def at_x(dx):
            return {"chan": lax.rem(x + dx + NX, NX) * nz + z}

        def at_z(dz):
            return {"chan": x * nz + lax.rem(z + dz + nz, nz)}

        def at_ctx(c):
            return {"ctx": c}

        def at_y(dy):
            return {"ctx": lax.rem(y + dy + ny, ny) * 2 + core}

        other = at_ctx(y * 2 + 1 - core)
        sign = 1 - 2 * core

        def remote(src, dst, ssem, rsem, device):
            return pltpu.make_async_remote_copy(
                src_ref=src, dst_ref=dst, send_sem=ssem, recv_sem=rsem,
                device_id=device, device_id_type=MESH)

        barrier = pltpu.get_barrier_semaphore()

        def greet(d, carry):
            pl.semaphore_signal(barrier, inc=1, device_id=at_ctx(lax.rem(ctx + d, nctx)),
                                device_id_type=MESH)
            return carry

        lax.fori_loop(1, nctx, greet, 0)
        for dx in range(1, NX):
            pl.semaphore_signal(barrier, inc=1, device_id=at_x(dx), device_id_type=MESH)
        for dz in strides:
            pl.semaphore_signal(barrier, inc=1, device_id=at_z(dz), device_id_type=MESH)

        loads = [pltpu.make_async_copy(s, d, in_sem.at[i]) for i, (s, d) in enumerate((
            (feat, feat_v), (ograd, og_v), (rate, rate_v), (residue, res_v), (sconv, sc_v),
            (sfilt, sf_v), (bias, bias_v)))]
        for c in loads:
            c.start()
        own_rows = pl.ds(pl.multiple_of(x * LANES, LANES), LANES)
        own_w = pltpu.make_async_copy(
            w.at[:, :, pl.ds(pl.multiple_of(x * width, LANES), width)],
            wbuf.at[:, own_rows, :], w_sem.at[0])
        own_w.start()
        for c in loads:
            c.wait()

        sig_v[...] = og_v[...] * feat_v[0]
        prod_v[...] = feat_v[1] * feat_v[2]

        iota8 = lax.broadcasted_iota(jnp.int32, (8, LANES), 0).astype(F32)
        for m in range(MODES):
            rm = jnp.broadcast_to(rate_v[m:m + 1, :], (8, LANES))
            d8 = jnp.exp(rm * -8.0)
            up = jnp.exp(-rm * iota8)
            base_v[m] = jnp.exp(-rm * (8.0 - iota8))
            d8_v[m] = d8
            total = jnp.zeros((8, LANES), F32)
            for k in range(blocks):
                total = total + up * sig_v[8 * k:8 * k + 8, :]
                up = up * d8
            fsend[m:m + 1, :] = jnp.sum(total, axis=0, keepdims=True)

        pl.semaphore_wait(barrier, nctx - 1 + NX - 1 + len(strides))

        prev = at_ctx(lax.rem(ctx + nctx - 1, nctx))
        halo_copies = [
            remote(feat.at[:, 0:8, :], halo.at[0:3], h_ssem.at[0], h_rsem.at[0], prev),
            remote(ograd.at[0:8, :], halo.at[3], h_ssem.at[1], h_rsem.at[1], prev),
            remote(sconv.at[0:8, :], halo.at[4], h_ssem.at[2], h_rsem.at[2], prev)]

        def f_copy(src_ctx, dst):
            return remote(fsend, frecv.at[src_ctx], f_ssem.at[dst], f_rsem.at[src_ctx], at_ctx(dst))

        for c in halo_copies:
            c.start()
        for dy in sorted(range(1, ny), key=lambda d: -min(d, ny - d)):
            @pl.when(y >= dy)
            def _():
                f_copy(ctx, (y - dy) * 2 + core).start()
                f_copy(ctx, (y - dy) * 2 + 1 - core).start()

        @pl.when(core == 1)
        def _():
            f_copy(ctx, y * 2).start()

        share = 2 * lax.rem(y, 2) + core
        r0 = share * share_rows

        def rows_of(dx, first, count):
            return pl.ds(pl.multiple_of(lax.rem(x + dx + NX, NX) * LANES + first, 8), count)

        def cols_of(dx, q):
            first = lax.rem(x + dx + NX, NX) * width + PARTS[q][1] * part
            return pl.ds(pl.multiple_of(first, LANES), PARTS[q][2] * part)

        mine = pl.ds(pl.multiple_of(r0, 8), share_rows)
        ry = (2 * (1 - lax.rem(y, 2)) + core) * share_rows
        towards = (2, 1, -1)
        origin = (2, -1, 1)

        def b_fetch(q, j):
            return remote(w.at[PARTS[q][0], mine, cols_of(towards[j], q)],
                          wbuf.at[PARTS[q][0], rows_of(0, r0, share_rows), cols_in(q)],
                          b_ssem.at[0, q, j], b_rsem.at[0, q, j], at_x(towards[j]))

        def cols_in(q):
            return pl.ds(PARTS[q][1] * part, PARTS[q][2] * part)

        def same_place(kind, q, j, first, count, device):
            ref = wbuf.at[PARTS[q][0], rows_of(origin[j], first, count), cols_in(q)]
            return remote(ref, ref, b_ssem.at[kind, q, j], b_rsem.at[kind, q, j], device)

        def b_core(p, j):
            return same_place(1, p, j, r0, share_rows, other)

        def b_up(p, j):
            return same_place(2, p, j, r0, half_rows, at_y(1))

        def b_down(p, j):
            return same_place(3, p, j, r0 + half_rows, half_rows, at_y(-1))

        def b_up_in(p, j):
            return same_place(2, p, j, ry, half_rows, at_y(1))

        def b_down_in(p, j):
            return same_place(3, p, j, ry + half_rows, half_rows, at_y(-1))

        def b_core2(p, j):
            return same_place(4, p, j, ry, share_rows, other)

        pieces = [(q, j) for q in range(len(PARTS)) for j in range(3)]
        for p, j in pieces:
            b_fetch(p, j).start()

        def fetched(p, j):
            b_fetch(p, j).wait_recv()
            b_up(p, j).start()
            b_down(p, j).start()
            b_core(p, j).start()

        def from_y(p, j):
            b_up_in(p, j).wait_recv()
            b_down_in(p, j).wait_recv()
            b_core2(p, j).start()

        dec = jnp.exp(-rate_v[...])
        res = res_v[...]

        def scan_block(i, carry):
            state, total = carry
            first = pl.multiple_of(TOK - 8 - 8 * i, 8)
            sig8 = sig_v[pl.ds(first, 8), :]
            prod8 = prod_v[pl.ds(first, 8), :]
            rows = [None] * 8
            for t in range(7, -1, -1):
                state = sig8[t:t + 1, :] + dec * state
                total = total + prod8[t:t + 1, :] * state
                rows[t] = jnp.sum(res * state, axis=0, keepdims=True)
            corr_v[pl.ds(first, 8), :] = jnp.concatenate(rows, axis=0)
            return state, total

        zero = jnp.zeros((MODES, LANES), F32)
        _, near_grad = lax.fori_loop(0, blocks, scan_block, (zero, zero))

        for m in range(MODES):
            down = base_v[m]
            d8 = d8_v[m]
            total = jnp.zeros((8, LANES), F32)
            for k in range(blocks - 1, -1, -1):
                total = total + down * prod_v[8 * k:8 * k + 8, :]
                down = down * d8
            z_v[m:m + 1, :] = jnp.sum(total, axis=0, keepdims=True)

        bias_row = bias_v[...]
        for c in halo_copies:
            c.wait_recv()
        keep = jnp.logical_and(ctx < nctx - 1, lax.broadcasted_iota(jnp.int32, (8, LANES), 0) < 2)
        sig_h = halo[3] * halo[0]
        prod_h = halo[1] * halo[2]
        gs_v[0, TOK:TOK + 8, :] = jnp.where(keep, halo[3] * (halo[4] + bias_row * prod_h), 0.0)
        gs_v[0, 0:TOK, :] = og_v[...] * (sc_v[...] + bias_row * prod_v[...])

        def finish_stream(p):
            taps = sf_v[p]
            g = taps[0:1, :] * gs_v[p, 0:TOK, :]
            g = g + taps[1:2, :] * gs_v[p, 1:TOK + 1, :]
            g = g + taps[2:3, :] * gs_v[p, 2:TOK + 2, :]
            gi_out[p] = g
            abuf[z, p] = g.astype(BF16)

        reach = (half, half - 1)

        def a_send(way, dist, p):
            heading = sign if way == 0 else -sign
            hops = dist if dist == JUMP[p] else 1
            ref = abuf.at[lax.rem(z - heading * (dist - hops) + nz, nz), p]
            return remote(ref, ref, a_ssem.at[way, dist, p], a_rsem.at[way, dist, p], at_z(heading * hops))

        def a_recv(way, dist, p):
            heading = sign if way == 0 else -sign
            ref = abuf.at[lax.rem(z - heading * dist + nz, nz), p]
            return remote(ref, ref, a_ssem.at[way, dist, p], a_rsem.at[way, dist, p], at_z(heading))

        def start_own(p):
            for dist in sorted({1, JUMP[p]}, reverse=p > 0):
                for way in range(2):
                    if dist <= reach[way]:
                        a_send(way, dist, p).start()

        def passes(way, dist, p):
            return dist + 1 <= reach[way] and dist + 1 != JUMP[p]

        def ring(p, dist):
            for way in range(2):
                if passes(way, dist, p):
                    a_recv(way, dist, p).wait_recv()
                    a_send(way, dist + 1, p).start()

        def ring_ends(p):
            for way in range(2):
                for dist in range(1, reach[way] + 1):
                    if not passes(way, dist, p):
                        a_recv(way, dist, p).wait_recv()

        finish_stream(0)
        start_own(0)

        for dist in range(1, EARLY + 1):
            ring(0, dist)

        d128 = jnp.exp(-rate_v[...] * float(TOK))

        def join(i, state):
            s = nctx - 1 - i
            f_copy(s, ctx).wait_recv()
            return frecv[s] + d128 * state

        state_in = lax.fori_loop(0, nctx - 1 - ctx, join, zero)

        q = res * state_in
        far = [jnp.zeros((8, LANES), F32) for _ in range(blocks)]
        for m in range(MODES):
            cur = q[m:m + 1, :] * base_v[m]
            d8 = d8_v[m]
            for k in range(blocks - 1, -1, -1):
                far[k] = far[k] + cur
                if k:
                    cur = cur * d8
        corr = corr_v[...] + jnp.concatenate(far, axis=0)
        corr_h0 = jnp.sum(q, axis=0, keepdims=True)
        state_h1 = (state_in - sig_h[0:1, :]) * jnp.exp(rate_v[...])
        corr_h1 = jnp.sum(res * state_h1, axis=0, keepdims=True)
        first_row = lax.broadcasted_iota(jnp.int32, (8, LANES), 0) == 0
        gp_h = jnp.where(first_row, corr_h0, corr_h1) + bias_row * sig_h
        gp = corr + bias_row * sig_v[...]
        gs_v[1, TOK:TOK + 8, :] = jnp.where(keep, gp_h * halo[2], 0.0)
        gs_v[1, 0:TOK, :] = gp * feat_v[2]
        finish_stream(1)
        start_own(1)
        gs_v[2, TOK:TOK + 8, :] = jnp.where(keep, gp_h * halo[1], 0.0)
        gs_v[2, 0:TOK, :] = gp * feat_v[1]
        finish_stream(2)
        start_own(2)

        gsum[0, 0:MODES, :] = near_grad + state_in * z_v[...]
        gsum[0, MODES:MODES + 8, :] = jnp.broadcast_to(
            jnp.sum(sig_v[...] * prod_v[...], axis=0, keepdims=True), (8, LANES))

        g_pair = remote(gsum.at[0], grecv.at[ny], g_ssem.at[0], g_rsem.at[0], other)
        g_pair.start()

        def g_copy(src, dy):
            return remote(gsum.at[1], grecv.at[src], g_ssem.at[dy], g_rsem.at[1 + src], at_y(dy))

        def g_chip():
            g_pair.wait_recv()
            chip = gsum[0] + grecv[ny]
            gsum[1] = chip
            grecv[y] = chip
            for dy in range(1, ny):
                g_copy(y, dy).start()

        events = []
        for dist in range(1, half + 1):
            for p in range(3):
                took = HOP * (dist if dist < JUMP[p] else dist - JUMP[p] + 0.7 + 0.3 * JUMP[p])
                if p or dist > EARLY:
                    events.append((A_START[p] + took, lambda p=p, dist=dist: ring(p, dist)))
        before = 0
        for q, (_, _, size) in enumerate(PARTS):
            for j in range(3):
                at = X_START + 18.3 / 48 * (before + size * (0.8, 0.95, 1.0)[j])
                events.append((at, lambda q=q, j=j: fetched(q, j)))
                events.append((at + 3.0 + 13.7 / 48 * size, lambda q=q, j=j: from_y(q, j)))
            before += size
        events.append((A_START[2] + 3.0, g_chip))
        for _, act in sorted(events, key=lambda e: e[0]):
            act()

        own_w.wait()
        dims = (((1,), (1,)), ((), ()))

        def product_of(p):
            for q, j in pieces:
                if PARTS[q][0] == p:
                    b_core(q, j).wait_recv()
                    b_core2(q, j).wait_recv()
            ring_ends(p)
            column = jnp.concatenate([abuf[slot, p] for slot in range(nz)], axis=1)
            return lax.dot_general(column, wbuf[p], dims, preferred_element_type=F32)

        acc_v[...] = product_of(0) + product_of(1)
        acc_v[...] += product_of(2)

        def piece(dx):
            return acc_v[:, pl.ds(pl.multiple_of(lax.rem(x + dx, NX) * LANES, LANES), LANES)]

        c_copies = []
        for dx in (2, 1, 3):
            csend[dx - 1] = piece(dx).astype(BF16)
            c = remote(csend.at[dx - 1], crecv.at[dx - 1], c_ssem.at[dx - 1], c_rsem.at[dx - 1], at_x(dx))
            c.start()
            c_copies.append(c)

        for src in range(1, ny):
            s = lax.rem(y + src, ny)
            g_copy(s, src).wait_recv()
        total = grecv[0]
        for src in range(1, ny):
            total = total + grecv[src]
        gr_out[...] = total[0:MODES, :] * scale
        gb_out[...] = total[MODES:MODES + 1, :] * scale

        for c in c_copies:
            c.wait_recv()
        gx_out[...] = ((piece(0) + crecv[0].astype(F32)) + crecv[1].astype(F32)) + crecv[2].astype(F32)

        for c in halo_copies + c_copies:
            c.wait_send()
        for p, j in pieces:
            for make in (b_fetch, b_core, b_up, b_down, b_core2):
                make(p, j).wait_send()
        g_pair.wait_send()
        for dy in range(1, ny):
            g_copy(y, dy).wait_send()

        def f_sent(i, carry):
            f_copy(ctx, i).wait_send()
            return carry

        lax.fori_loop(0, ctx, f_sent, 0)

        for p in range(3):
            for way in range(2):
                for dist in range(1, reach[way] + 1):
                    a_send(way, dist, p).wait_send()

    return kernel


def build(nctx, nchan):
    nz = nchan // NX
    half = nz // 2
    width = nz * LANES
    ny = nctx // 2
    any_spec = pl.BlockSpec(memory_space=pl.ANY)
    vmem_spec = pl.BlockSpec(memory_space=pltpu.VMEM)
    dma = pltpu.SemaphoreType.DMA
    vm = pltpu.VMEM
    shapes = (
        jax.ShapeDtypeStruct((3, TOK, LANES), F32),
        jax.ShapeDtypeStruct((TOK, LANES), F32),
        jax.ShapeDtypeStruct((MODES, LANES), F32),
        jax.ShapeDtypeStruct((1, LANES), F32))
    call = pl.pallas_call(
        make_kernel(nctx, nz),
        out_shape=shapes,
        in_specs=[any_spec] * 8,
        out_specs=(vmem_spec,) * 4,
        scratch_shapes=[
            vm((3, TOK, LANES), F32), vm((TOK, LANES), F32), vm((TOK, LANES), F32),
            vm((3, 3, LANES), F32), vm((MODES, LANES), F32), vm((MODES, LANES), F32), vm((1, LANES), F32),
            vm((TOK, LANES), F32), vm((TOK, LANES), F32), vm((TOK, LANES), F32), vm((3, TOK + 8, LANES), F32),
            vm((MODES, 8, LANES), F32), vm((MODES, 8, LANES), F32), vm((MODES, LANES), F32),
            vm((MODES, LANES), F32), vm((nctx, MODES, LANES), F32), vm((5, 8, LANES), F32),
            vm((2, MODES + 8, LANES), F32), vm((ny + 1, MODES + 8, LANES), F32),
            vm((nz, 3, TOK, LANES), BF16), vm((3, NX * LANES, width), BF16),
            vm((TOK, NX * LANES), F32), vm((NX - 1, TOK, LANES), BF16), vm((NX - 1, TOK, LANES), BF16),
            dma((7,)), dma((1,)), dma((nctx,)), dma((nctx,)), dma((3,)), dma((3,)), dma((ny,)), dma((ny + 1,)),
            dma((2, nz // 2 + 1, 3)), dma((2, nz // 2 + 1, 3)), dma((5, len(PARTS), 3)), dma((5, len(PARTS), 3)), dma((3,)), dma((3,))],
        compiler_params=pltpu.CompilerParams(
            collective_id=0, has_side_effects=True, vmem_limit_bytes=40 * 1024 * 1024),
    )

    def put_out_kernel(*refs):
        sources, targets, sem = refs[:4], refs[4:8], refs[8]
        copies = [pltpu.make_async_copy(a, b, sem.at[i]) for i, (a, b) in enumerate(zip(sources, targets))]
        for c in copies:
            c.start()
        for c in copies:
            c.wait()

    put_out = pl.pallas_call(
        put_out_kernel,
        out_shape=shapes,
        in_specs=[vmem_spec] * 4,
        out_specs=(any_spec,) * 4,
        scratch_shapes=[dma((4,))],
        compiler_params=pltpu.CompilerParams(vmem_limit_bytes=8 * 1024 * 1024),
    )

    def body(features, saved_conv, out_grad, short_filter, residue, rate, bias, w_proj):
        operands = (features, saved_conv, out_grad, short_filter, residue.T, rate.T, bias.reshape(1, LANES), w_proj)
        gi, gx, gr, gb = put_out(*call(*[pltpu.with_memory_space_constraint(v, pltpu.HBM) for v in operands]))
        return gi, gx, gr.T, gb.reshape(LANES)

    return body


def solution(mesh):
    return jax.shard_map(
        build(mesh.shape["ctx"], mesh.shape["chan"]),
        mesh=mesh,
        in_specs=(
            P(None, "ctx", "chan"),
            P("ctx", "chan"),
            P("ctx", "chan"),
            P(None, None, "chan"),
            P("chan", None),
            P("chan", None),
            P("chan"),
            P(None, "chan", None),
        ),
        out_specs=(P(None, "ctx", "chan"), P("ctx", "chan"), P("chan", None), P("chan")),
        check_vma=False,
    )
```

```python
import jax
import jax.numpy as jnp
from jax import lax
from jax.experimental import pallas as pl
from jax.experimental.pallas import tpu as pltpu
from jax.sharding import PartitionSpec as P

NX = 4
MODES = 16
TOK = 128
LANES = 128
SHARES = 4
PARTS = ((0, 0, 16), (1, 0, 16), (2, 0, 8), (2, 8, 4), (2, 12, 4))
X_START, HOP, A_START = 7.7, 4.0, (9.0, 13.0, 13.3)
JUMP = (4, 4, 4)
EARLY = 1
F32 = jnp.float32
BF16 = jnp.bfloat16
MESH = pl.DeviceIdType.MESH


def make_kernel(nctx, nz):
    ny = nctx // 2
    half = nz // 2
    strides = [way * d for d in sorted({1} | {j for j in JUMP if j <= half}) for way in (1, -1)]
    width = nz * LANES
    part = width // 16
    share_rows = LANES // SHARES
    half_rows = share_rows // 2
    scale = (TOK * nctx) ** -0.5
    blocks = TOK // 8

    def kernel(feat, sconv, ograd, sfilt, residue, rate, bias, w,
               gi_out, gx_out, gr_out, gb_out,
               feat_v, sc_v, og_v, sf_v, res_v, rate_v, bias_v, sig_v, prod_v, corr_v, gs_v,
               base_v, d8_v, z_v, fsend, frecv, halo, gsum, grecv, abuf, wbuf,
               acc_v, csend, crecv,
               in_sem, w_sem, f_ssem, f_rsem, h_ssem, h_rsem, g_ssem, g_rsem,
               a_ssem, a_rsem, b_ssem, b_rsem, c_ssem, c_rsem):
        ctx = lax.axis_index("ctx")
        chan = lax.axis_index("chan")
        x = chan // nz
        z = lax.rem(chan, nz)
        y = ctx // 2
        core = lax.rem(ctx, 2)

        def at_x(dx):
            return {"chan": lax.rem(x + dx + NX, NX) * nz + z}

        def at_z(dz):
            return {"chan": x * nz + lax.rem(z + dz + nz, nz)}

        def at_ctx(c):
            return {"ctx": c}

        def at_y(dy):
            return {"ctx": lax.rem(y + dy + ny, ny) * 2 + core}

        other = at_ctx(y * 2 + 1 - core)
        sign = 1 - 2 * core

        def remote(src, dst, ssem, rsem, device):
            return pltpu.make_async_remote_copy(
                src_ref=src, dst_ref=dst, send_sem=ssem, recv_sem=rsem,
                device_id=device, device_id_type=MESH)

        barrier = pltpu.get_barrier_semaphore()

        def greet(d, carry):
            pl.semaphore_signal(barrier, inc=1, device_id=at_ctx(lax.rem(ctx + d, nctx)),
                                device_id_type=MESH)
            return carry

        lax.fori_loop(1, nctx, greet, 0)
        for dx in range(1, NX):
            pl.semaphore_signal(barrier, inc=1, device_id=at_x(dx), device_id_type=MESH)
        for dz in strides:
            pl.semaphore_signal(barrier, inc=1, device_id=at_z(dz), device_id_type=MESH)

        loads = [pltpu.make_async_copy(s, d, in_sem.at[i]) for i, (s, d) in enumerate((
            (feat, feat_v), (ograd, og_v), (rate, rate_v), (residue, res_v), (sconv, sc_v),
            (sfilt, sf_v), (bias, bias_v)))]
        for c in loads:
            c.start()
        own_rows = pl.ds(pl.multiple_of(x * LANES, LANES), LANES)
        own_w = pltpu.make_async_copy(
            w.at[:, :, pl.ds(pl.multiple_of(x * width, LANES), width)],
            wbuf.at[:, own_rows, :], w_sem.at[0])
        own_w.start()
        for c in loads:
            c.wait()

        sig_v[...] = og_v[...] * feat_v[0]
        prod_v[...] = feat_v[1] * feat_v[2]

        iota8 = lax.broadcasted_iota(jnp.int32, (8, LANES), 0).astype(F32)
        for m in range(MODES):
            rm = jnp.broadcast_to(rate_v[m:m + 1, :], (8, LANES))
            d8 = jnp.exp(rm * -8.0)
            up = jnp.exp(-rm * iota8)
            base_v[m] = jnp.exp(-rm * (8.0 - iota8))
            d8_v[m] = d8
            total = jnp.zeros((8, LANES), F32)
            for k in range(blocks):
                total = total + up * sig_v[8 * k:8 * k + 8, :]
                up = up * d8
            fsend[m:m + 1, :] = jnp.sum(total, axis=0, keepdims=True)

        pl.semaphore_wait(barrier, nctx - 1 + NX - 1 + len(strides))

        prev = at_ctx(lax.rem(ctx + nctx - 1, nctx))
        halo_copies = [
            remote(feat.at[:, 0:8, :], halo.at[0:3], h_ssem.at[0], h_rsem.at[0], prev),
            remote(ograd.at[0:8, :], halo.at[3], h_ssem.at[1], h_rsem.at[1], prev),
            remote(sconv.at[0:8, :], halo.at[4], h_ssem.at[2], h_rsem.at[2], prev)]

        def f_copy(src_ctx, dst):
            return remote(fsend, frecv.at[src_ctx], f_ssem.at[dst], f_rsem.at[src_ctx], at_ctx(dst))

        for c in halo_copies:
            c.start()
        for dy in sorted(range(1, ny), key=lambda d: -min(d, ny - d)):
            @pl.when(y >= dy)
            def _():
                f_copy(ctx, (y - dy) * 2 + core).start()
                f_copy(ctx, (y - dy) * 2 + 1 - core).start()

        @pl.when(core == 1)
        def _():
            f_copy(ctx, y * 2).start()

        share = 2 * lax.rem(y, 2) + core
        r0 = share * share_rows

        def rows_of(dx, first, count):
            return pl.ds(pl.multiple_of(lax.rem(x + dx + NX, NX) * LANES + first, 8), count)

        def cols_of(dx, q):
            first = lax.rem(x + dx + NX, NX) * width + PARTS[q][1] * part
            return pl.ds(pl.multiple_of(first, LANES), PARTS[q][2] * part)

        mine = pl.ds(pl.multiple_of(r0, 8), share_rows)
        ry = (2 * (1 - lax.rem(y, 2)) + core) * share_rows
        towards = (2, 1, -1)
        origin = (2, -1, 1)

        def b_fetch(q, j):
            return remote(w.at[PARTS[q][0], mine, cols_of(towards[j], q)],
                          wbuf.at[PARTS[q][0], rows_of(0, r0, share_rows), cols_in(q)],
                          b_ssem.at[0, q, j], b_rsem.at[0, q, j], at_x(towards[j]))

        def cols_in(q):
            return pl.ds(PARTS[q][1] * part, PARTS[q][2] * part)

        def same_place(kind, q, j, first, count, device):
            ref = wbuf.at[PARTS[q][0], rows_of(origin[j], first, count), cols_in(q)]
            return remote(ref, ref, b_ssem.at[kind, q, j], b_rsem.at[kind, q, j], device)

        def b_core(p, j):
            return same_place(1, p, j, r0, share_rows, other)

        def b_up(p, j):
            return same_place(2, p, j, r0, half_rows, at_y(1))

        def b_down(p, j):
            return same_place(3, p, j, r0 + half_rows, half_rows, at_y(-1))

        def b_up_in(p, j):
            return same_place(2, p, j, ry, half_rows, at_y(1))

        def b_down_in(p, j):
            return same_place(3, p, j, ry + half_rows, half_rows, at_y(-1))

        def b_core2(p, j):
            return same_place(4, p, j, ry, share_rows, other)

        pieces = [(q, j) for q in range(len(PARTS)) for j in range(3)]
        for p, j in pieces:
            b_fetch(p, j).start()

        def fetched(p, j):
            b_fetch(p, j).wait_recv()
            b_up(p, j).start()
            b_down(p, j).start()
            b_core(p, j).start()

        def from_y(p, j):
            b_up_in(p, j).wait_recv()
            b_down_in(p, j).wait_recv()
            b_core2(p, j).start()

        dec = jnp.exp(-rate_v[...])
        res = res_v[...]

        def scan_block(i, carry):
            state, total = carry
            first = pl.multiple_of(TOK - 8 - 8 * i, 8)
            sig8 = sig_v[pl.ds(first, 8), :]
            prod8 = prod_v[pl.ds(first, 8), :]
            rows = [None] * 8
            for t in range(7, -1, -1):
                state = sig8[t:t + 1, :] + dec * state
                total = total + prod8[t:t + 1, :] * state
                rows[t] = jnp.sum(res * state, axis=0, keepdims=True)
            corr_v[pl.ds(first, 8), :] = jnp.concatenate(rows, axis=0)
            return state, total

        zero = jnp.zeros((MODES, LANES), F32)
        _, near_grad = lax.fori_loop(0, blocks, scan_block, (zero, zero))

        for m in range(MODES):
            down = base_v[m]
            d8 = d8_v[m]
            total = jnp.zeros((8, LANES), F32)
            for k in range(blocks - 1, -1, -1):
                total = total + down * prod_v[8 * k:8 * k + 8, :]
                down = down * d8
            z_v[m:m + 1, :] = jnp.sum(total, axis=0, keepdims=True)

        bias_row = bias_v[...]
        for c in halo_copies:
            c.wait_recv()
        keep = jnp.logical_and(ctx < nctx - 1, lax.broadcasted_iota(jnp.int32, (8, LANES), 0) < 2)
        sig_h = halo[3] * halo[0]
        prod_h = halo[1] * halo[2]
        gs_v[0, TOK:TOK + 8, :] = jnp.where(keep, halo[3] * (halo[4] + bias_row * prod_h), 0.0)
        gs_v[0, 0:TOK, :] = og_v[...] * (sc_v[...] + bias_row * prod_v[...])

        def finish_stream(p):
            taps = sf_v[p]
            g = taps[0:1, :] * gs_v[p, 0:TOK, :]
            g = g + taps[1:2, :] * gs_v[p, 1:TOK + 1, :]
            g = g + taps[2:3, :] * gs_v[p, 2:TOK + 2, :]
            gi_out[p] = g
            abuf[z, p] = g.astype(BF16)

        reach = (half, half - 1)

        def a_send(way, dist, p):
            heading = sign if way == 0 else -sign
            hops = dist if dist == JUMP[p] else 1
            ref = abuf.at[lax.rem(z - heading * (dist - hops) + nz, nz), p]
            return remote(ref, ref, a_ssem.at[way, dist, p], a_rsem.at[way, dist, p], at_z(heading * hops))

        def a_recv(way, dist, p):
            heading = sign if way == 0 else -sign
            ref = abuf.at[lax.rem(z - heading * dist + nz, nz), p]
            return remote(ref, ref, a_ssem.at[way, dist, p], a_rsem.at[way, dist, p], at_z(heading))

        def start_own(p):
            for dist in sorted({1, JUMP[p]}):
                for way in range(2):
                    if dist <= reach[way]:
                        a_send(way, dist, p).start()

        def passes(way, dist, p):
            return dist + 1 <= reach[way] and dist + 1 != JUMP[p]

        def ring(p, dist):
            for way in range(2):
                if passes(way, dist, p):
                    a_recv(way, dist, p).wait_recv()
                    a_send(way, dist + 1, p).start()

        def ring_ends(p):
            for way in range(2):
                for dist in range(1, reach[way] + 1):
                    if not passes(way, dist, p):
                        a_recv(way, dist, p).wait_recv()

        finish_stream(0)
        start_own(0)

        for dist in range(1, EARLY + 1):
            ring(0, dist)

        d128 = jnp.exp(-rate_v[...] * float(TOK))

        def join(i, state):
            s = nctx - 1 - i
            f_copy(s, ctx).wait_recv()
            return frecv[s] + d128 * state

        state_in = lax.fori_loop(0, nctx - 1 - ctx, join, zero)

        q = res * state_in
        far = [jnp.zeros((8, LANES), F32) for _ in range(blocks)]
        for m in range(MODES):
            cur = q[m:m + 1, :] * base_v[m]
            d8 = d8_v[m]
            for k in range(blocks - 1, -1, -1):
                far[k] = far[k] + cur
                if k:
                    cur = cur * d8
        corr = corr_v[...] + jnp.concatenate(far, axis=0)
        corr_h0 = jnp.sum(q, axis=0, keepdims=True)
        state_h1 = (state_in - sig_h[0:1, :]) * jnp.exp(rate_v[...])
        corr_h1 = jnp.sum(res * state_h1, axis=0, keepdims=True)
        first_row = lax.broadcasted_iota(jnp.int32, (8, LANES), 0) == 0
        gp_h = jnp.where(first_row, corr_h0, corr_h1) + bias_row * sig_h
        gp = corr + bias_row * sig_v[...]
        gs_v[1, TOK:TOK + 8, :] = jnp.where(keep, gp_h * halo[2], 0.0)
        gs_v[1, 0:TOK, :] = gp * feat_v[2]
        finish_stream(1)
        start_own(1)
        gs_v[2, TOK:TOK + 8, :] = jnp.where(keep, gp_h * halo[1], 0.0)
        gs_v[2, 0:TOK, :] = gp * feat_v[1]
        finish_stream(2)
        start_own(2)

        gsum[0, 0:MODES, :] = near_grad + state_in * z_v[...]
        gsum[0, MODES:MODES + 8, :] = jnp.broadcast_to(
            jnp.sum(sig_v[...] * prod_v[...], axis=0, keepdims=True), (8, LANES))

        g_pair = remote(gsum.at[0], grecv.at[ny], g_ssem.at[0], g_rsem.at[0], other)
        g_pair.start()

        def g_copy(src, dy):
            return remote(gsum.at[1], grecv.at[src], g_ssem.at[dy], g_rsem.at[1 + src], at_y(dy))

        def g_chip():
            g_pair.wait_recv()
            chip = gsum[0] + grecv[ny]
            gsum[1] = chip
            grecv[y] = chip
            for dy in range(1, ny):
                g_copy(y, dy).start()

        events = []
        for dist in range(1, half + 1):
            for p in range(3):
                took = HOP * (dist if dist < JUMP[p] else dist - JUMP[p] + 0.7 + 0.3 * JUMP[p])
                if p or dist > EARLY:
                    events.append((A_START[p] + took, lambda p=p, dist=dist: ring(p, dist)))
        before = 0
        for q, (_, _, size) in enumerate(PARTS):
            for j in range(3):
                at = X_START + 18.3 / 48 * (before + size * (0.8, 0.95, 1.0)[j])
                events.append((at, lambda q=q, j=j: fetched(q, j)))
                events.append((at + 3.0 + 13.7 / 48 * size, lambda q=q, j=j: from_y(q, j)))
            before += size
        events.append((A_START[2] + 3.0, g_chip))
        for _, act in sorted(events, key=lambda e: e[0]):
            act()

        own_w.wait()
        dims = (((1,), (1,)), ((), ()))

        def product_of(p):
            for q, j in pieces:
                if PARTS[q][0] == p:
                    b_core(q, j).wait_recv()
                    b_core2(q, j).wait_recv()
            ring_ends(p)
            column = jnp.concatenate([abuf[slot, p] for slot in range(nz)], axis=1)
            return lax.dot_general(column, wbuf[p], dims, preferred_element_type=F32)

        acc_v[...] = product_of(0) + product_of(1)
        acc_v[...] += product_of(2)

        def piece(dx):
            return acc_v[:, pl.ds(pl.multiple_of(lax.rem(x + dx, NX) * LANES, LANES), LANES)]

        c_copies = []
        for dx in (2, 1, 3):
            csend[dx - 1] = piece(dx).astype(BF16)
            c = remote(csend.at[dx - 1], crecv.at[dx - 1], c_ssem.at[dx - 1], c_rsem.at[dx - 1], at_x(dx))
            c.start()
            c_copies.append(c)

        for src in range(1, ny):
            s = lax.rem(y + src, ny)
            g_copy(s, src).wait_recv()
        total = grecv[0]
        for src in range(1, ny):
            total = total + grecv[src]
        gr_out[...] = total[0:MODES, :] * scale
        gb_out[...] = total[MODES:MODES + 1, :] * scale

        for c in c_copies:
            c.wait_recv()
        gx_out[...] = ((piece(0) + crecv[0].astype(F32)) + crecv[1].astype(F32)) + crecv[2].astype(F32)

        for c in halo_copies + c_copies:
            c.wait_send()
        for p, j in pieces:
            for make in (b_fetch, b_core, b_up, b_down, b_core2):
                make(p, j).wait_send()
        g_pair.wait_send()
        for dy in range(1, ny):
            g_copy(y, dy).wait_send()

        def f_sent(i, carry):
            f_copy(ctx, i).wait_send()
            return carry

        lax.fori_loop(0, ctx, f_sent, 0)

        for p in range(3):
            for way in range(2):
                for dist in range(1, reach[way] + 1):
                    a_send(way, dist, p).wait_send()

    return kernel


def build(nctx, nchan):
    nz = nchan // NX
    half = nz // 2
    width = nz * LANES
    ny = nctx // 2
    any_spec = pl.BlockSpec(memory_space=pl.ANY)
    vmem_spec = pl.BlockSpec(memory_space=pltpu.VMEM)
    dma = pltpu.SemaphoreType.DMA
    vm = pltpu.VMEM
    shapes = (
        jax.ShapeDtypeStruct((3, TOK, LANES), F32),
        jax.ShapeDtypeStruct((TOK, LANES), F32),
        jax.ShapeDtypeStruct((MODES, LANES), F32),
        jax.ShapeDtypeStruct((1, LANES), F32))
    call = pl.pallas_call(
        make_kernel(nctx, nz),
        out_shape=shapes,
        in_specs=[any_spec] * 8,
        out_specs=(vmem_spec,) * 4,
        scratch_shapes=[
            vm((3, TOK, LANES), F32), vm((TOK, LANES), F32), vm((TOK, LANES), F32),
            vm((3, 3, LANES), F32), vm((MODES, LANES), F32), vm((MODES, LANES), F32), vm((1, LANES), F32),
            vm((TOK, LANES), F32), vm((TOK, LANES), F32), vm((TOK, LANES), F32), vm((3, TOK + 8, LANES), F32),
            vm((MODES, 8, LANES), F32), vm((MODES, 8, LANES), F32), vm((MODES, LANES), F32),
            vm((MODES, LANES), F32), vm((nctx, MODES, LANES), F32), vm((5, 8, LANES), F32),
            vm((2, MODES + 8, LANES), F32), vm((ny + 1, MODES + 8, LANES), F32),
            vm((nz, 3, TOK, LANES), BF16), vm((3, NX * LANES, width), BF16),
            vm((TOK, NX * LANES), F32), vm((NX - 1, TOK, LANES), BF16), vm((NX - 1, TOK, LANES), BF16),
            dma((7,)), dma((1,)), dma((nctx,)), dma((nctx,)), dma((3,)), dma((3,)), dma((ny,)), dma((ny + 1,)),
            dma((2, nz // 2 + 1, 3)), dma((2, nz // 2 + 1, 3)), dma((5, len(PARTS), 3)), dma((5, len(PARTS), 3)), dma((3,)), dma((3,))],
        compiler_params=pltpu.CompilerParams(
            collective_id=0, has_side_effects=True, vmem_limit_bytes=40 * 1024 * 1024),
    )

    def put_out_kernel(*refs):
        sources, targets, sem = refs[:4], refs[4:8], refs[8]
        copies = [pltpu.make_async_copy(a, b, sem.at[i]) for i, (a, b) in enumerate(zip(sources, targets))]
        for c in copies:
            c.start()
        for c in copies:
            c.wait()

    put_out = pl.pallas_call(
        put_out_kernel,
        out_shape=shapes,
        in_specs=[vmem_spec] * 4,
        out_specs=(any_spec,) * 4,
        scratch_shapes=[dma((4,))],
        compiler_params=pltpu.CompilerParams(vmem_limit_bytes=8 * 1024 * 1024),
    )

    def body(features, saved_conv, out_grad, short_filter, residue, rate, bias, w_proj):
        operands = (features, saved_conv, out_grad, short_filter, residue.T, rate.T, bias.reshape(1, LANES), w_proj)
        gi, gx, gr, gb = put_out(*call(*[pltpu.with_memory_space_constraint(v, pltpu.HBM) for v in operands]))
        return gi, gx, gr.T, gb.reshape(LANES)

    return body


def solution(mesh):
    return jax.shard_map(
        build(mesh.shape["ctx"], mesh.shape["chan"]),
        mesh=mesh,
        in_specs=(
            P(None, "ctx", "chan"),
            P("ctx", "chan"),
            P("ctx", "chan"),
            P(None, None, "chan"),
            P("chan", None),
            P("chan", None),
            P("chan"),
            P(None, "chan", None),
        ),
        out_specs=(P(None, "ctx", "chan"), P("ctx", "chan"), P("chan", None), P("chan")),
        check_vma=False,
    )
```
